32 devices in a mesh: group: 2 (over x), tok: 16 (over z, y, core).
Axes of the slice: x: 2, y: 2, z: 4, core: 2. Of those that a mesh axis runs over, the one named last changes fastest.
Arguments:
- initial_guess: float32 [512, 16, 128], P(('group', 'tok')), parts along dimension 0, may hold values from -6 to 6
- noise_draws: float32 [512, 16, 128], P(('group', 'tok')), parts along dimension 0, may hold values from -6 to 6
- drift_state: float32 [16], replicated, may hold values from 0 to 0.15
- drift_denoise: float32 [16], replicated, may hold values from -0.4 to -0.15
- noise_scale: float32 [16], replicated, may hold values from 0.05 to 0.3
- modulation: float32 [16, 8, 1152], replicated, may hold values from -3 to 3
- embed_weight: bfloat16 [16, 1152], replicated, may hold values from -1.5 to 1.5
- space_input: bfloat16 [1152, 1728], replicated, may hold values from -0.1875 to 0.1875
- space_output: bfloat16 [576, 1152], replicated, may hold values from -0.25 to 0.25
- time_input: bfloat16 [1152, 1728], replicated, may hold values from -0.1875 to 0.1875
- time_output: bfloat16 [576, 1152], replicated, may hold values from -0.25 to 0.25
- final_weight: bfloat16 [1152, 16], replicated, may hold values from -0.1875 to 0.1875
Outputs:
- next_states: float32 [512, 16, 128], P(('group', 'tok')), parts along dimension 0
The draws below stay inside these ranges and needn't reach their ends.
There are 2 independent parts, one for each index of `group`. The reference program is written for one: setup_inputs(seed, part) draws one part's arguments, and reference() takes and returns one part's arrays. A program takes and returns all parts, laid end to end along the dimension named above; an argument that names none is the same for every part. Nothing has to cross between parts.
All inputs are finite; a program needn't handle non-finite values.
Results may differ from the reference program's by a relative error of at most 0.006.
Values may be sent and summed in bfloat16 or wider, within the bound.
A program may use at most 128 MiB of HBM per device.

```python
import jax
import jax.numpy as jnp
from jax import lax

D = 1152
HEADS = 8
HD = 72
LCH = 16
F = 16
P_SIZE = 16
ITERS = 2
HW = 128
INNER = 576
ROWS = 256


def steps_of(stream_key, shape, cuts, least, largest):
    gain, own = 1.0, jax.random.fold_in(stream_key, 6)
    for position, shards_of in cuts:
        steps = jnp.exp(jax.random.uniform(jax.random.fold_in(own, position), (shards_of,), jnp.float32, least / len(cuts), largest / len(cuts)))
        gain = gain * jnp.repeat(steps, shape[position] // shards_of).reshape([-1 if axis == position else 1 for axis in range(len(shape))])
    return gain


def centred(key, shape, spread, bound, shards=(), kind=jnp.bfloat16):
    values = spread * jax.random.normal(key, shape, jnp.float32)
    if shards:
        values = values * steps_of(key, shape, shards, -0.22, 0.18)
    return jnp.clip(values, -bound, bound).astype(kind)


def setup_inputs(seed: int = 0, part: int = 0) -> dict:
    arg_keys = jax.random.split(jax.random.key(seed), 13)
    part_splits = jax.random.split(jax.random.fold_in(arg_keys[12], part), 13)
    return {
        "initial_guess": centred(part_splits[0], (ROWS, LCH, HW), 1.0, 6.0, ((0, 16),), jnp.float32),
        "noise_draws": centred(part_splits[1], (ROWS, LCH, HW), 1.0, 6.0, ((0, 16),), jnp.float32),
        "drift_state": jnp.clip(jax.random.uniform(arg_keys[2], (P_SIZE,), jnp.float32, 0.0, 0.15), 0.0, 0.15),
        "drift_denoise": jnp.clip(jax.random.uniform(arg_keys[3], (P_SIZE,), jnp.float32, -0.4, -0.15), -0.4, -0.15),
        "noise_scale": jnp.clip(jax.random.uniform(arg_keys[4], (P_SIZE,), jnp.float32, 0.05, 0.3), 0.05, 0.3),
        "modulation": centred(arg_keys[5], (P_SIZE, 8, D), 0.4, 3.0, (), jnp.float32),
        "embed_weight": centred(arg_keys[6], (LCH, D), LCH ** -0.5, 1.5),
        "space_input": centred(arg_keys[7], (D, 3 * INNER), D ** -0.5, 0.1875),
        "space_output": centred(arg_keys[8], (INNER, D), INNER ** -0.5, 0.25),
        "time_input": centred(arg_keys[9], (D, 3 * INNER), D ** -0.5, 0.1875),
        "time_output": centred(arg_keys[10], (INNER, D), INNER ** -0.5, 0.25),
        "final_weight": centred(arg_keys[11], (D, LCH), D ** -0.5, 0.1875),
    }


def layer_norm(values):
    center = values - lax.optimization_barrier(jnp.mean(values, -1, keepdims=True))
    return center * lax.rsqrt(lax.optimization_barrier(jnp.mean(center * center, -1, keepdims=True)) + 1e-06)

def head_norm(values):
    return values * lax.rsqrt(lax.optimization_barrier(jnp.mean(values * values, -1, keepdims=True)) + 1e-06)

def attention_mix(normed, input_weight, output_weight):
    batches, length, feature_width = normed.shape
    packed = jnp.dot(normed.reshape(-1, feature_width), input_weight, preferred_element_type=jnp.float32)
    packed = packed.reshape(batches, length, 3, HEADS, HD)
    queries = head_norm(packed[:, :, 0]).astype(jnp.bfloat16)
    key_rows = head_norm(packed[:, :, 1]).astype(jnp.bfloat16)
    value_rows = packed[:, :, 2].astype(jnp.bfloat16)
    scores = jnp.einsum('blhe,bmhe->bhlm', queries.astype(jnp.float32), key_rows.astype(jnp.float32)) * HD ** (-0.5)
    weights = jnp.exp(scores)
    weights = (weights / lax.optimization_barrier(jnp.sum(weights, -1, keepdims=True))).astype(jnp.bfloat16)
    attended = jnp.einsum('bhlm,bmhe->blhe', weights.astype(jnp.float32), value_rows.astype(jnp.float32)).astype(jnp.bfloat16)
    result = jnp.dot(attended.reshape(-1, HEADS * HD), output_weight, preferred_element_type=jnp.float32)
    return result.reshape(batches, length, feature_width)

def denoiser(latent, modulation_row, embed_weight, space_input, space_output, time_input, time_output, final_weight):
    embedded = jnp.einsum('fch,cd->fhd', latent.astype(jnp.bfloat16).astype(jnp.float32), embed_weight.astype(jnp.float32))
    normed = (layer_norm(embedded) * (1.0 + modulation_row[1]) + modulation_row[0]).astype(jnp.bfloat16)
    after_space = (embedded + modulation_row[2] * attention_mix(normed, space_input, space_output)).astype(jnp.bfloat16)
    after_space = lax.optimization_barrier(after_space)
    hidden = jnp.swapaxes(after_space, 0, 1).astype(jnp.float32)
    normed = (layer_norm(hidden) * (1.0 + modulation_row[4]) + modulation_row[3]).astype(jnp.bfloat16)
    after_time = (hidden + modulation_row[5] * attention_mix(normed, time_input, time_output)).astype(jnp.bfloat16)
    after_time = lax.optimization_barrier(after_time).astype(jnp.float32)
    normed = (layer_norm(after_time) * (1.0 + modulation_row[7]) + modulation_row[6]).astype(jnp.bfloat16)
    return jnp.einsum('hfd,dc->fch', normed.astype(jnp.float32), final_weight.astype(jnp.float32))

def reference(initial_guess, noise_draws, drift_state, drift_denoise, noise_scale, modulation, embed_weight, space_input, space_output, time_input, time_output, final_weight):
    latent = initial_guess.reshape(P_SIZE, F, LCH, HW)
    fresh_noise = noise_draws.reshape(P_SIZE, F, LCH, HW)
    leading = (jnp.arange(P_SIZE) == 0)[:, None, None, None]
    rate_state = drift_state[:, None, None, None]
    rate_denoise = drift_denoise[:, None, None, None]
    rate_noise = noise_scale[:, None, None, None]
    running = latent
    for iteration in range(ITERS):
        predicted = lax.map(lambda paired: denoiser(paired[0], paired[1], embed_weight, space_input, space_output, time_input, time_output, final_weight), (latent, modulation))
        increment = rate_state * latent + rate_denoise * predicted + rate_noise * fresh_noise
        increment = jnp.where(leading, increment + latent, increment)
        running = jnp.cumsum(increment, axis=0)
        latent = jnp.concatenate([latent[:1], running[:-1]], axis=0)
    return running.reshape(ROWS, LCH, HW)
```

```python
import functools
import math

import jax
import jax.numpy as jnp
from jax import lax
from jax.experimental import pallas as pl
from jax.experimental.pallas import tpu as pltpu
from jax.sharding import PartitionSpec as P

HEADS = 8
HD = 72
P_SIZE = 16
ITERS = 2
LANES = 128
INNER = HEADS * HD
PADDED = -(-INNER // LANES) * LANES
BLOCK_TOKENS = 256


def layer_norm(values):
    center = values - jnp.mean(values, -1, keepdims=True)
    return center * lax.rsqrt(jnp.mean(center * center, -1, keepdims=True) + 1e-06)


def head_slab(head):
    first = head * HD // LANES
    last = (head * HD + HD - 1) // LANES
    return first, last - first + 1


def attend(read, write, rows, keep):
    lane = lax.broadcasted_iota(jnp.int32, (rows, LANES), 1)
    outs = []
    for head in range(HEADS):
        tile, tiles = head_slab(head)
        low = head * HD - tile * LANES
        width = tiles * LANES
        lanes = lax.broadcasted_iota(jnp.int32, (rows, width), 1)
        inside = (lanes >= low) & (lanes < low + HD)
        queries = jnp.where(inside, read(0, tile, tiles), 0.0)
        keys = jnp.where(inside, read(1, tile, tiles), 0.0)
        values = read(2, tile, tiles).astype(jnp.bfloat16)
        query_rate = lax.rsqrt(jnp.sum(queries * queries, -1, keepdims=True) / HD + 1e-06)
        key_rate = lax.rsqrt(jnp.sum(keys * keys, -1, keepdims=True) / HD + 1e-06)
        queries = (queries * (query_rate * (HD**-0.5 * math.log2(math.e)))).astype(jnp.bfloat16)
        keys = (keys * key_rate).astype(jnp.bfloat16)
        scores = lax.dot_general(
            queries, keys, (((1,), (1,)), ((), ())), preferred_element_type=jnp.float32
        )
        weights = jnp.exp2(scores)
        if keep is not None:
            weights = jnp.where(keep, weights, 0.0)
        weights = weights * (1.0 / jnp.sum(weights, -1, keepdims=True))
        outs.append(
            jnp.dot(weights.astype(jnp.bfloat16), values, preferred_element_type=jnp.float32)
        )
    for tile in range(PADDED // LANES):
        total = None
        for head in range(HEADS):
            first, tiles = head_slab(head)
            if first <= tile < first + tiles:
                part = outs[head][:, (tile - first) * LANES : (tile - first + 1) * LANES]
                if total is None:
                    total = part
                else:
                    total = jnp.where(lane >= head * HD - tile * LANES, part, total)
        write(tile, total)


def space_kernel(
    latent_ref, table_ref, embed_ref, input_ref, output_ref, after_ref,
    embedded_ref, packed_ref, mixed_ref,
):
    frames, channels, spatial = latent_ref.shape
    for frame in range(frames):
        embedded_ref[frame * spatial : (frame + 1) * spatial, :] = lax.dot_general(
            latent_ref[frame].astype(jnp.bfloat16),
            embed_ref[...],
            (((0,), (0,)), ((), ())),
            preferred_element_type=jnp.float32,
        )
    normed = (
        layer_norm(embedded_ref[...]) * (1.0 + table_ref[1:2, :]) + table_ref[0:1, :]
    ).astype(jnp.bfloat16)
    packed_ref[...] = jnp.dot(normed, input_ref[...], preferred_element_type=jnp.float32)

    def one(frame, carry):
        rows = pl.ds(pl.multiple_of(frame * spatial, spatial), spatial)

        def read(part, tile, tiles):
            return packed_ref[rows, part * PADDED + tile * LANES : part * PADDED + (tile + tiles) * LANES]

        def write(tile, values):
            mixed_ref[rows, tile * LANES : (tile + 1) * LANES] = values

        attend(read, write, spatial, None)
        return carry

    lax.fori_loop(0, frames, one, 0)
    result = jnp.dot(
        mixed_ref[...].astype(jnp.bfloat16), output_ref[...], preferred_element_type=jnp.float32
    )
    after = (embedded_ref[...] + table_ref[2:3, :] * result).astype(jnp.bfloat16)
    after_ref[...] = after.reshape(after_ref.shape)


def time_kernel(
    after_ref, table_ref, input_ref, output_ref, final_ref, predicted_ref, packed_ref, mixed_ref
):
    frames, positions, width = after_ref.shape
    chunk = 8
    tokens = frames * positions
    rows = frames * chunk
    hidden = after_ref[...].reshape(tokens, width).astype(jnp.float32)
    normed = (layer_norm(hidden) * (1.0 + table_ref[4:5, :]) + table_ref[3:4, :]).astype(
        jnp.bfloat16
    )
    packed_ref[...] = jnp.dot(
        normed, input_ref[...], preferred_element_type=jnp.float32
    ).reshape(packed_ref.shape)
    keep = (lax.broadcasted_iota(jnp.int32, (rows, rows), 0) % chunk) == (
        lax.broadcasted_iota(jnp.int32, (rows, rows), 1) % chunk
    )

    def one(index, carry):
        own = pl.ds(pl.multiple_of(index * chunk, chunk), chunk)

        def read(part, tile, tiles):
            block = packed_ref[
                :, own, part * PADDED + tile * LANES : part * PADDED + (tile + tiles) * LANES
            ]
            return block.reshape(rows, tiles * LANES)

        def write(tile, values):
            mixed_ref[:, own, tile * LANES : (tile + 1) * LANES] = values.reshape(
                frames, chunk, LANES
            )

        attend(read, write, rows, keep)
        return carry

    lax.fori_loop(0, positions // chunk, one, 0)
    mixed = mixed_ref[...].reshape(tokens, PADDED).astype(jnp.bfloat16)
    result = jnp.dot(mixed, output_ref[...], preferred_element_type=jnp.float32)
    hidden = after_ref[...].reshape(tokens, width).astype(jnp.float32)
    settled = (hidden + table_ref[5:6, :] * result).astype(jnp.bfloat16).astype(jnp.float32)
    normed = (layer_norm(settled) * (1.0 + table_ref[7:8, :]) + table_ref[6:7, :]).astype(
        jnp.bfloat16
    )
    predicted = jnp.dot(normed, final_ref[...], preferred_element_type=jnp.float32)
    predicted_ref[...] = predicted.reshape(predicted_ref.shape)


def whole(array):
    zeros = (0,) * array.ndim
    return pl.BlockSpec(array.shape, lambda step: zeros, pipeline_mode=pl.Buffered(1))


def space_block(latent, table, embed_weight, input_weight, output_weight):
    frames, channels, spatial = latent.shape
    width = embed_weight.shape[1]
    step_frames = math.gcd(frames, max(1, BLOCK_TOKENS // spatial))
    tokens = step_frames * spatial
    return pl.pallas_call(
        space_kernel,
        grid=(frames // step_frames,),
        out_shape=jax.ShapeDtypeStruct((frames, spatial, width), jnp.bfloat16),
        in_specs=[
            pl.BlockSpec((step_frames, channels, spatial), lambda step: (step, 0, 0)),
            whole(table),
            whole(embed_weight),
            whole(input_weight),
            whole(output_weight),
        ],
        out_specs=pl.BlockSpec((step_frames, spatial, width), lambda step: (step, 0, 0)),
        scratch_shapes=[
            pltpu.VMEM((tokens, width), jnp.float32),
            pltpu.VMEM((tokens, 3 * PADDED), jnp.float32),
            pltpu.VMEM((tokens, PADDED), jnp.float32),
        ],
        compiler_params=pltpu.CompilerParams(vmem_limit_bytes=40 * 1024 * 1024),
        name="space_block",
    )(latent, table, embed_weight, input_weight, output_weight)


def time_block(after, table, input_weight, output_weight, final_weight):
    frames, positions, width = after.shape
    channels = final_weight.shape[1]
    step_positions = math.gcd(positions, max(16, BLOCK_TOKENS // frames))
    return pl.pallas_call(
        time_kernel,
        grid=(positions // step_positions,),
        out_shape=jax.ShapeDtypeStruct((frames, positions, channels), jnp.float32),
        in_specs=[
            pl.BlockSpec((frames, step_positions, width), lambda step: (0, step, 0)),
            whole(table),
            whole(input_weight),
            whole(output_weight),
            whole(final_weight),
        ],
        out_specs=pl.BlockSpec((frames, step_positions, channels), lambda step: (0, step, 0)),
        scratch_shapes=[
            pltpu.VMEM((frames, step_positions, 3 * PADDED), jnp.float32),
            pltpu.VMEM((frames, step_positions, PADDED), jnp.float32),
        ],
        compiler_params=pltpu.CompilerParams(vmem_limit_bytes=40 * 1024 * 1024),
        name="time_block",
    )(after, table, input_weight, output_weight, final_weight)


def pad_input(weight):
    width = weight.shape[0]
    parts = weight.reshape(width, 3, INNER)
    return jnp.pad(parts, ((0, 0), (0, 0), (0, PADDED - INNER))).reshape(width, 3 * PADDED)


def pad_output(weight):
    return jnp.pad(weight, ((0, PADDED - INNER), (0, 0)))


def body(
    initial_guess,
    noise_draws,
    drift_state,
    drift_denoise,
    noise_scale,
    modulation,
    embed_weight,
    space_input,
    space_output,
    time_input,
    time_output,
    final_weight,
):
    devices = lax.axis_size("tok")
    own_index = lax.axis_index("tok")
    groups = devices // P_SIZE
    timestep = own_index // groups
    leading = timestep == 0
    table = lax.dynamic_index_in_dim(modulation, timestep, 0, keepdims=False)
    rate_state = lax.dynamic_index_in_dim(drift_state, timestep, 0, keepdims=False)
    rate_denoise = lax.dynamic_index_in_dim(drift_denoise, timestep, 0, keepdims=False)
    rate_noise = lax.dynamic_index_in_dim(noise_scale, timestep, 0, keepdims=False)
    space_in, space_out = pad_input(space_input), pad_output(space_output)
    time_in, time_out = pad_input(time_input), pad_output(time_output)
    same_step = [[step * groups + block for block in range(groups)] for step in range(P_SIZE)]
    same_block = [[step * groups + block for step in range(P_SIZE)] for block in range(groups)]
    latent = initial_guess
    result = initial_guess
    for iteration in range(ITERS):
        after = space_block(latent, table, embed_weight, space_in, space_out)
        if groups > 1:
            after = lax.all_to_all(
                after, "tok", split_axis=1, concat_axis=0, axis_index_groups=same_step, tiled=True
            )
        predicted = time_block(after, table, time_in, time_out, final_weight)
        predicted = jnp.swapaxes(predicted, 1, 2)
        if groups > 1:
            predicted = lax.all_to_all(
                predicted, "tok", split_axis=0, concat_axis=2, axis_index_groups=same_step, tiled=True
            )
        increment = rate_state * latent + rate_denoise * predicted + rate_noise * noise_draws
        increment = jnp.where(leading, increment + latent, increment)
        gathered = lax.all_gather(
            increment.astype(jnp.bfloat16),
            "tok",
            axis_index_groups=same_block if groups > 1 else None,
        )
        earlier = (jnp.arange(P_SIZE) < timestep)[:, None, None, None]
        before = jnp.sum(jnp.where(earlier, gathered.astype(jnp.float32), 0.0), axis=0)
        result = before + increment
        latent = jnp.where(leading, latent, before)
    return result


def solution(mesh):
    placed = (
        P(("group", "tok"), None, None),
        P(("group", "tok"), None, None),
        P(),
        P(),
        P(),
        P(),
        P(),
        P(),
        P(),
        P(),
        P(),
        P(),
    )
    return jax.shard_map(
        body, mesh=mesh, in_specs=placed, out_specs=P(("group", "tok"), None, None), check_vma=False
    )
```

```python
import functools
import math

import jax
import jax.numpy as jnp
from jax import lax
from jax.experimental import pallas as pl
from jax.experimental.pallas import tpu as pltpu
from jax.sharding import PartitionSpec as P

HEADS = 8
HD = 72
P_SIZE = 16
ITERS = 2
LANES = 128
INNER = HEADS * HD
PADDED = -(-INNER // LANES) * LANES
BLOCK_TOKENS = 256
SIDE = math.isqrt(P_SIZE)


def layer_norm(values):
    center = values - jnp.mean(values, -1, keepdims=True)
    return center * lax.rsqrt(jnp.mean(center * center, -1, keepdims=True) + 1e-06)


def head_slab(head):
    first = head * HD // LANES
    last = (head * HD + HD - 1) // LANES
    return first, last - first + 1


def part_lanes(part, tile, tiles):
    if part == 1:
        return 1, tile * LANES, (tile + tiles) * LANES
    start = part * INNER
    return 0, start + tile * LANES, start + min((tile + tiles) * LANES, INNER if part else PADDED)


def lined_keys(packed):
    low = INNER // LANES * LANES
    return pltpu.roll(packed[:, low : low + PADDED], PADDED - (INNER - low), 1)


def attend(read, write, rows, keep):
    lane = lax.broadcasted_iota(jnp.int32, (rows, LANES), 1)
    outs = []
    for head in range(HEADS):
        tile, tiles = head_slab(head)
        low = head * HD - tile * LANES
        width = tiles * LANES
        lanes = lax.broadcasted_iota(jnp.int32, (rows, width), 1)
        inside = (lanes >= low) & (lanes < low + HD)
        queries = jnp.where(inside, read(0, tile, tiles), 0.0)
        keys = jnp.where(inside, read(1, tile, tiles), 0.0)
        values = read(2, tile, tiles).astype(jnp.bfloat16)
        query_rate = lax.rsqrt(jnp.sum(queries * queries, -1, keepdims=True) / HD + 1e-06)
        key_rate = lax.rsqrt(jnp.sum(keys * keys, -1, keepdims=True) / HD + 1e-06)
        queries = (queries * (query_rate * (HD**-0.5 * math.log2(math.e)))).astype(jnp.bfloat16)
        keys = (keys * key_rate).astype(jnp.bfloat16)
        scores = lax.dot_general(
            queries, keys, (((1,), (1,)), ((), ())), preferred_element_type=jnp.float32
        )
        weights = jnp.exp2(scores)
        if keep is not None:
            weights = jnp.where(keep, weights, 0.0)
        weights = weights * (1.0 / jnp.sum(weights, -1, keepdims=True))
        outs.append(
            jnp.dot(weights.astype(jnp.bfloat16), values, preferred_element_type=jnp.float32)
        )
    for tile in range(PADDED // LANES):
        total = None
        for head in range(HEADS):
            first, tiles = head_slab(head)
            if first <= tile < first + tiles:
                part = outs[head][:, (tile - first) * LANES : (tile - first + 1) * LANES]
                if total is None:
                    total = part
                else:
                    total = jnp.where(lane >= head * HD - tile * LANES, part, total)
        write(tile, total)


def space_kernel(
    step_ref, latent_ref, table_ref, embed_ref, input_ref, output_ref, after_ref,
    embedded_ref, packed_ref, key_ref, mixed_ref,
):
    frames, channels, spatial = latent_ref.shape
    for frame in range(frames):
        embedded_ref[frame * spatial : (frame + 1) * spatial, :] = lax.dot_general(
            latent_ref[frame].astype(jnp.bfloat16),
            embed_ref[...],
            (((0,), (0,)), ((), ())),
            preferred_element_type=jnp.float32,
        )
    normed = (
        layer_norm(embedded_ref[...]) * (1.0 + table_ref[1:2, :]) + table_ref[0:1, :]
    ).astype(jnp.bfloat16)
    packed = jnp.dot(normed, input_ref[...], preferred_element_type=jnp.float32)
    packed_ref[...] = packed
    key_ref[...] = lined_keys(packed)

    def one(frame, carry):
        rows = pl.ds(pl.multiple_of(frame * spatial, spatial), spatial)

        def read(part, tile, tiles):
            source, start, stop = part_lanes(part, tile, tiles)
            return (packed_ref, key_ref)[source][rows, start:stop]

        def write(tile, values):
            mixed_ref[rows, tile * LANES : tile * LANES + values.shape[1]] = values

        attend(read, write, spatial, None)
        return carry

    lax.fori_loop(0, frames, one, 0)
    result = jnp.dot(
        mixed_ref[...].astype(jnp.bfloat16), output_ref[...], preferred_element_type=jnp.float32
    )
    after = (embedded_ref[...] + table_ref[2:3, :] * result).astype(jnp.bfloat16)
    after_ref[...] = after.reshape(after_ref.shape)


def time_kernel(fused, *refs):
    step_ref, after_ref, table_ref, input_ref, output_ref, final_ref, *refs = refs
    if fused:
        latent_ref, noise_ref, *rate_refs, increment_ref, sent_ref = refs[:7]
    else:
        result_ref = refs[0]
    predicted_ref, packed_ref, key_ref, mixed_ref = refs[-4:]
    frames, positions, width = after_ref.shape
    chunk = 8
    tokens = frames * positions
    rows = frames * chunk
    hidden = after_ref[...].reshape(tokens, width).astype(jnp.float32)
    normed = (layer_norm(hidden) * (1.0 + table_ref[4:5, :]) + table_ref[3:4, :]).astype(
        jnp.bfloat16
    )
    packed = jnp.dot(normed, input_ref[...], preferred_element_type=jnp.float32)
    packed_ref[...] = packed.reshape(packed_ref.shape)
    key_ref[...] = lined_keys(packed).reshape(key_ref.shape)
    keep = (lax.broadcasted_iota(jnp.int32, (rows, rows), 0) % chunk) == (
        lax.broadcasted_iota(jnp.int32, (rows, rows), 1) % chunk
    )

    def one(index, carry):
        own = pl.ds(pl.multiple_of(index * chunk, chunk), chunk)

        def read(part, tile, tiles):
            source, start, stop = part_lanes(part, tile, tiles)
            return (packed_ref, key_ref)[source][:, own, start:stop].reshape(rows, stop - start)

        def write(tile, values):
            lanes = values.shape[1]
            mixed_ref[:, own, tile * LANES : tile * LANES + lanes] = values.reshape(
                frames, chunk, lanes
            )

        attend(read, write, rows, keep)
        return carry

    lax.fori_loop(0, positions // chunk, one, 0)
    mixed = mixed_ref[...].reshape(tokens, INNER).astype(jnp.bfloat16)
    result = jnp.dot(mixed, output_ref[...], preferred_element_type=jnp.float32)
    hidden = after_ref[...].reshape(tokens, width).astype(jnp.float32)
    settled = (hidden + table_ref[5:6, :] * result).astype(jnp.bfloat16).astype(jnp.float32)
    normed = (layer_norm(settled) * (1.0 + table_ref[7:8, :]) + table_ref[6:7, :]).astype(
        jnp.bfloat16
    )
    predicted = jnp.dot(normed, final_ref[...], preferred_element_type=jnp.float32)
    own = pl.ds(pl.multiple_of(pl.program_id(0) * positions, positions), positions)
    predicted_ref[:, own, :] = predicted.reshape(frames, positions, predicted.shape[1])

    @pl.when(pl.program_id(0) == pl.num_programs(0) - 1)
    def _():
        if fused:
            timestep = step_ref[0]
            rate_state, rate_denoise, rate_noise = (ref[timestep] for ref in rate_refs)
            rate_state = rate_state + jnp.where(timestep == 0, 1.0, 0.0)
        for frame in range(frames):
            turned = predicted_ref[frame].T
            if fused:
                turned = (
                    rate_state * latent_ref[frame]
                    + rate_denoise * turned
                    + rate_noise * noise_ref[frame]
                )
                increment_ref[frame] = turned
                sent_ref[frame] = turned.astype(jnp.bfloat16)
            else:
                result_ref[frame] = turned


def whole(array):
    zeros = (0,) * array.ndim
    return pl.BlockSpec(array.shape, lambda step, *_: zeros, pipeline_mode=pl.Buffered(1))


def own_row(modulation):
    return pl.BlockSpec(
        (None,) + modulation.shape[1:],
        lambda step, own: (own[0], 0, 0),
        pipeline_mode=pl.Buffered(1),
    )


def cost_of(tokens, *weights):
    return pl.CostEstimate(
        flops=2 * tokens * sum(weight.size for weight in weights),
        bytes_accessed=2 * sum(weight.size for weight in weights) + 4 * tokens * weights[0].shape[0],
        transcendentals=0,
    )


def space_block(own, latent, modulation, embed_weight, input_weight, output_weight):
    frames, channels, spatial = latent.shape
    width = embed_weight.shape[1]
    step_frames = math.gcd(frames, max(1, BLOCK_TOKENS // spatial))
    tokens = step_frames * spatial
    return pl.pallas_call(
        space_kernel,
        out_shape=jax.ShapeDtypeStruct((frames, spatial, width), jnp.bfloat16),
        grid_spec=pltpu.PrefetchScalarGridSpec(
            num_scalar_prefetch=1,
            grid=(frames // step_frames,),
            in_specs=[
                pl.BlockSpec((step_frames, channels, spatial), lambda step, own: (step, 0, 0)),
                own_row(modulation),
                whole(embed_weight),
                whole(input_weight),
                whole(output_weight),
            ],
            out_specs=pl.BlockSpec((step_frames, spatial, width), lambda step, own: (step, 0, 0)),
            scratch_shapes=[
                pltpu.VMEM((tokens, width), jnp.float32),
                pltpu.VMEM((tokens, 3 * INNER), jnp.float32),
                pltpu.VMEM((tokens, PADDED), jnp.float32),
                pltpu.VMEM((tokens, INNER), jnp.float32),
            ],
        ),
        compiler_params=pltpu.CompilerParams(vmem_limit_bytes=36 * 1024 * 1024),
        cost_estimate=cost_of(frames * spatial, input_weight, output_weight, output_weight),
        name="space_block",
    )(own, latent, modulation, embed_weight, input_weight, output_weight)


def time_block(own, after, modulation, input_weight, output_weight, final_weight, fused=()):
    frames, positions, width = after.shape
    channels = final_weight.shape[1]
    step_positions = math.gcd(positions, max(16, BLOCK_TOKENS // frames))
    shape = (frames, channels, positions)
    kinds = [jnp.float32] + [jnp.bfloat16] * bool(fused)
    return pl.pallas_call(
        functools.partial(time_kernel, bool(fused)),
        out_shape=[jax.ShapeDtypeStruct(shape, kind) for kind in kinds],
        grid_spec=pltpu.PrefetchScalarGridSpec(
            num_scalar_prefetch=1,
            grid=(positions // step_positions,),
            in_specs=[
                pl.BlockSpec((frames, step_positions, width), lambda step, own: (0, step, 0)),
                own_row(modulation),
                whole(input_weight),
                whole(output_weight),
                whole(final_weight),
            ]
            + [
                whole(array) if array.ndim > 1 else pl.BlockSpec(memory_space=pltpu.SMEM)
                for array in fused
            ],
            out_specs=[
                pl.BlockSpec(shape, lambda step, own: (0, 0, 0), pipeline_mode=pl.Buffered(1))
                for kind in kinds
            ],
            scratch_shapes=[
                pltpu.VMEM((frames, positions, channels), jnp.float32),
                pltpu.VMEM((frames, step_positions, 3 * INNER), jnp.float32),
                pltpu.VMEM((frames, step_positions, PADDED), jnp.float32),
                pltpu.VMEM((frames, step_positions, INNER), jnp.float32),
            ],
        ),
        compiler_params=pltpu.CompilerParams(vmem_limit_bytes=36 * 1024 * 1024),
        cost_estimate=cost_of(frames * positions, input_weight, output_weight, output_weight),
        name="time_block",
    )(own, after, modulation, input_weight, output_weight, final_weight, *fused)


def carry_kernel(
    last, groups, sent_ref, increment_ref, latent_ref, out_ref,
    part_ref, total_ref, plane_ref, early_ref, stage_ref, before_ref,
    part_send, part_recv, plane_send, plane_recv, stage_send, stage_recv,
):
    quarter = part_ref.shape[1]
    own = lax.axis_index("tok")
    timestep = own // groups
    plane, seat = timestep // SIDE, timestep % SIDE

    def device(plane, seat):
        return {"tok": (plane * SIDE + seat) * groups + own % groups}

    def seat_after(hop):
        return (seat + hop) % SIDE

    barrier = pltpu.get_barrier_semaphore()
    for hop in range(1, SIDE):
        for target in (device(plane, seat_after(hop)), device((plane + hop) % SIDE, seat)):
            pl.semaphore_signal(
                barrier, inc=1, device_id=target, device_id_type=pl.DeviceIdType.MESH
            )
    pl.semaphore_wait(barrier, 2 * (SIDE - 1))

    def copy(source, target, send, receive, to):
        return pltpu.make_async_remote_copy(
            src_ref=source,
            dst_ref=target,
            send_sem=send,
            recv_sem=receive,
            device_id=to,
            device_id_type=pl.DeviceIdType.MESH,
        )

    def rows_of(index):
        return pl.ds(pl.multiple_of(index * quarter, quarter), quarter)

    parts = []
    for hop in range(1, SIDE):
        seat_to = seat_after(hop)
        parts.append(
            copy(
                sent_ref.at[rows_of(seat_to)], part_ref.at[hop - 1],
                part_send.at[hop - 1], part_recv.at[hop - 1], device(plane, seat_to),
            )
        )
        parts[-1].start()
    held = [sent_ref[rows_of(seat)].astype(jnp.float32)]
    for hop in range(1, SIDE):
        parts[hop - 1].wait_recv()
        held.append(part_ref[hop - 1].astype(jnp.float32))
    total_ref[...] = functools.reduce(jnp.add, held).astype(jnp.bfloat16)
    planes = [
        copy(
            total_ref, plane_ref.at[hop - 1], plane_send.at[hop - 1], plane_recv.at[hop - 1],
            device((plane + hop) % SIDE, seat),
        )
        for hop in range(1, SIDE)
    ]
    for hop in range(1, SIDE):
        pl.when(plane + hop < SIDE)(planes[hop - 1].start)

    def earlier_seats(limit):
        total = jnp.zeros_like(held[0])
        for hop in range(SIDE):
            total = total + jnp.where((seat + SIDE - hop) % SIDE < limit, held[hop], 0.0)
        return total

    early_ref[...] = jnp.zeros_like(early_ref)
    for hop in range(1, SIDE):

        @pl.when(plane >= hop)
        def _(hop=hop):
            planes[hop - 1].wait_recv()
            early_ref[...] += plane_ref[hop - 1].astype(jnp.float32)

    early = early_ref[...]
    stages = []
    for hop in range(1, SIDE):
        seat_to = seat_after(hop)
        stage_ref[hop - 1] = early + earlier_seats(seat_to)
        stages.append(
            copy(
                stage_ref.at[hop - 1], before_ref.at[rows_of(seat)],
                stage_send.at[hop - 1], stage_recv.at[hop - 1], device(plane, seat_to),
            )
        )
        stages[-1].start()
    own_rows = rows_of(seat)

    def settle(rows, before):
        if last:
            out_ref[rows] = before + increment_ref[rows]
        else:
            out_ref[rows] = jnp.where(timestep == 0, latent_ref[rows], before)

    settle(own_rows, early + earlier_seats(seat))
    for hop in range(1, SIDE):
        stages[hop - 1].wait_recv()
        rows = rows_of((seat + SIDE - hop) % SIDE)
        settle(rows, before_ref[rows])
    for hop in range(1, SIDE):
        parts[hop - 1].wait_send()
        pl.when(plane + hop < SIDE)(planes[hop - 1].wait_send)
        stages[hop - 1].wait_send()


def carried_kernel(last, groups, sent, increment, latent):
    rows, lanes = sent.shape
    quarter = rows // SIDE
    hops = SIDE - 1
    vmem = pl.BlockSpec(memory_space=pltpu.VMEM)
    return pl.pallas_call(
        functools.partial(carry_kernel, last, groups),
        out_shape=jax.ShapeDtypeStruct((rows, lanes), jnp.float32),
        in_specs=[vmem] * 3,
        out_specs=vmem,
        scratch_shapes=[
            pltpu.VMEM((hops, quarter, lanes), jnp.bfloat16),
            pltpu.VMEM((quarter, lanes), jnp.bfloat16),
            pltpu.VMEM((hops, quarter, lanes), jnp.bfloat16),
            pltpu.VMEM((quarter, lanes), jnp.float32),
            pltpu.VMEM((hops, quarter, lanes), jnp.float32),
            pltpu.VMEM((rows, lanes), jnp.float32),
        ]
        + [pltpu.SemaphoreType.DMA((hops,))] * 6,
        compiler_params=pltpu.CompilerParams(collective_id=int(last), has_side_effects=True),
        name="carry_last" if last else "carry",
    )(sent, increment, latent)


def carried_in(last, groups, same_block, timestep, sent, increment, latent):
    rows = sent.size // LANES
    if sent.shape[-1] == LANES and rows % (SIDE * 16) == 0:
        flat = [array.reshape(rows, LANES) for array in (sent, increment, latent)]
        return carried_kernel(last, groups, *flat).reshape(latent.shape)
    gathered = lax.all_gather(
        sent, "tok", axis_index_groups=same_block if groups > 1 else None
    )
    earlier = (jnp.arange(P_SIZE) < timestep)[:, None, None, None]
    before = jnp.sum(jnp.where(earlier, gathered.astype(jnp.float32), 0.0), axis=0)
    return before + increment if last else jnp.where(timestep == 0, latent, before)


def body(
    initial_guess,
    noise_draws,
    drift_state,
    drift_denoise,
    noise_scale,
    modulation,
    embed_weight,
    space_input,
    space_output,
    time_input,
    time_output,
    final_weight,
):
    devices = lax.axis_size("tok")
    own_index = lax.axis_index("tok")
    groups = devices // P_SIZE
    timestep = own_index // groups
    own = jnp.reshape(timestep, (1,)).astype(jnp.int32)
    rates = (drift_state, drift_denoise, noise_scale)
    same_step = [[step * groups + block for block in range(groups)] for step in range(P_SIZE)]
    same_block = [[step * groups + block for step in range(P_SIZE)] for block in range(groups)]
    latent = initial_guess
    for iteration in range(ITERS):
        after = space_block(own, latent, modulation, embed_weight, space_input, space_output)
        if groups == 1:
            increment, sent = time_block(
                own, after, modulation, time_input, time_output, final_weight,
                (latent, noise_draws) + rates,
            )
        else:
            after = lax.all_to_all(
                after, "tok", split_axis=1, concat_axis=0, axis_index_groups=same_step, tiled=True
            )
            (predicted,) = time_block(own, after, modulation, time_input, time_output, final_weight)
            predicted = lax.all_to_all(
                predicted, "tok", split_axis=0, concat_axis=2, axis_index_groups=same_step, tiled=True
            )
            rate_state, rate_denoise, rate_noise = (
                lax.dynamic_index_in_dim(rate, timestep, 0, keepdims=False) for rate in rates
            )
            rate_state = rate_state + jnp.where(timestep == 0, 1.0, 0.0)
            increment = rate_state * latent + rate_denoise * predicted + rate_noise * noise_draws
            sent = increment.astype(jnp.bfloat16)
        latent = carried_in(
            iteration == ITERS - 1, groups, same_block, timestep, sent, increment, latent
        )
    return latent


def solution(mesh):
    placed = (
        P(("group", "tok"), None, None),
        P(("group", "tok"), None, None),
        P(),
        P(),
        P(),
        P(),
        P(),
        P(),
        P(),
        P(),
        P(),
        P(),
    )
    return jax.shard_map(
        body, mesh=mesh, in_specs=placed, out_specs=P(("group", "tok"), None, None), check_vma=False
    )
```

```python
import functools
import math

import jax
import jax.numpy as jnp
from jax import lax
from jax.experimental import pallas as pl
from jax.experimental.pallas import tpu as pltpu
from jax.sharding import PartitionSpec as P

HEADS = 8
HD = 72
P_SIZE = 16
ITERS = 2
LANES = 128
INNER = HEADS * HD
PADDED = -(-INNER // LANES) * LANES
BLOCK_TOKENS = 256
SIDE = math.isqrt(P_SIZE)


def layer_norm(values):
    center = values - jnp.mean(values, -1, keepdims=True)
    return center * lax.rsqrt(jnp.mean(center * center, -1, keepdims=True) + 1e-06)


def dot_rows(values, weight_rows):
    return lax.dot_general(
        values, weight_rows, (((1,), (1,)), ((), ())), preferred_element_type=jnp.float32
    )


def head_slab(head):
    first = head * HD // LANES
    last = (head * HD + HD - 1) // LANES
    return first, last - first + 1


def part_lanes(part, tile, tiles):
    if part == 1:
        return 1, tile * LANES, (tile + tiles) * LANES
    start = part * INNER
    return 0, start + tile * LANES, start + min((tile + tiles) * LANES, INNER if part else PADDED)


def lined_keys(packed):
    low = INNER // LANES * LANES
    return pltpu.roll(packed[:, low : low + PADDED], PADDED - (INNER - low), 1)


def attend(blocks, rows, keep):
    lane = lax.broadcasted_iota(jnp.int32, (rows, LANES), 1)
    open_tiles = {}
    units = [(head, place) for head in range(HEADS) for place in range(len(blocks))]

    def prepare(unit):
        head, place = unit
        read = blocks[place][0]
        tile, tiles = head_slab(head)
        low = head * HD - tile * LANES
        lanes = lax.broadcasted_iota(jnp.int32, (rows, tiles * LANES), 1)
        inside = (lanes >= low) & (lanes < low + HD)
        queries = jnp.where(inside, read(0, tile, tiles), 0.0)
        keys = jnp.where(inside, read(1, tile, tiles), 0.0)
        query_rate = lax.rsqrt(jnp.sum(queries * queries, -1, keepdims=True) / HD + 1e-06)
        key_rate = lax.rsqrt(jnp.sum(keys * keys, -1, keepdims=True) / HD + 1e-06)
        queries = (queries * (query_rate * (HD**-0.5 * math.log2(math.e)))).astype(jnp.bfloat16)
        return queries, (keys * key_rate).astype(jnp.bfloat16)

    def weigh(unit, prepared):
        weights = jnp.exp2(dot_rows(*prepared))
        if keep is not None:
            weights = jnp.where(keep, weights, 0.0)
        return (weights * (1.0 / jnp.sum(weights, -1, keepdims=True))).astype(jnp.bfloat16)

    def mix(unit, weights):
        head, place = unit
        read, write = blocks[place]
        tile, tiles = head_slab(head)
        values = read(2, tile, tiles).astype(jnp.bfloat16)
        mixed = jnp.dot(weights, values, preferred_element_type=jnp.float32)
        for own in range(tile, tile + tiles):
            part = mixed[:, (own - tile) * LANES : (own - tile + 1) * LANES]
            if (place, own) in open_tiles:
                part = jnp.where(
                    lane >= head * HD - own * LANES, part, open_tiles.pop((place, own))
                )
            if (head + 1) * HD >= min((own + 1) * LANES, INNER):
                write(own, part)
            else:
                open_tiles[place, own] = part

    prepared, weighed = {}, {}
    for at in range(len(units) + 8):
        if at < len(units):
            prepared[at] = prepare(units[at])
        if 0 <= at - 4 < len(units):
            weighed[at - 4] = weigh(units[at - 4], prepared.pop(at - 4))
        if 0 <= at - 8 < len(units):
            mix(units[at - 8], weighed.pop(at - 8))


def space_kernel(
    step_ref, latent_ref, table_ref, embed_ref, input_ref, output_ref, after_ref,
    embedded_ref, packed_ref, key_ref, mixed_ref,
):
    frames, channels, spatial = latent_ref.shape
    for frame in range(frames):
        embedded_ref[frame * spatial : (frame + 1) * spatial, :] = lax.dot_general(
            latent_ref[frame].astype(jnp.bfloat16),
            embed_ref[...],
            (((0,), (0,)), ((), ())),
            preferred_element_type=jnp.float32,
        )
    normed = (
        layer_norm(embedded_ref[...]) * (1.0 + table_ref[1:2, :]) + table_ref[0:1, :]
    ).astype(jnp.bfloat16)
    packed = dot_rows(normed, input_ref[...])
    packed_ref[...] = packed
    key_ref[...] = lined_keys(packed)

    def one(frame):
        rows = slice(frame * spatial, (frame + 1) * spatial)

        def read(part, tile, tiles):
            source, start, stop = part_lanes(part, tile, tiles)
            return (packed_ref, key_ref)[source][rows, start:stop]

        def write(tile, values):
            mixed_ref[rows, tile * LANES : tile * LANES + values.shape[1]] = values

        return read, write

    attend([one(frame) for frame in range(frames)], spatial, None)
    result = jnp.dot(
        mixed_ref[...].astype(jnp.bfloat16), output_ref[...], preferred_element_type=jnp.float32
    )
    after = (embedded_ref[...] + table_ref[2:3, :] * result).astype(jnp.bfloat16)
    after_ref[...] = after.reshape(after_ref.shape)


def time_kernel(fused, *refs):
    step_ref, after_ref, table_ref, input_ref, output_ref, final_ref, *refs = refs
    if fused:
        latent_ref, noise_ref, *rate_refs, increment_ref, sent_ref = refs[:7]
    else:
        result_ref = refs[0]
    predicted_ref, packed_ref, key_ref, mixed_ref = refs[-4:]
    frames, positions, width = after_ref.shape
    chunk = 8
    tokens = frames * positions
    rows = frames * chunk
    hidden = after_ref[...].reshape(tokens, width).astype(jnp.float32)
    normed = (layer_norm(hidden) * (1.0 + table_ref[4:5, :]) + table_ref[3:4, :]).astype(
        jnp.bfloat16
    )
    packed = dot_rows(normed, input_ref[...])
    packed_ref[...] = packed.reshape(packed_ref.shape)
    key_ref[...] = lined_keys(packed).reshape(key_ref.shape)
    keep = (lax.broadcasted_iota(jnp.int32, (rows, rows), 0) % chunk) == (
        lax.broadcasted_iota(jnp.int32, (rows, rows), 1) % chunk
    )

    def one(index):
        own = slice(index * chunk, (index + 1) * chunk)

        def read(part, tile, tiles):
            source, start, stop = part_lanes(part, tile, tiles)
            return (packed_ref, key_ref)[source][:, own, start:stop].reshape(rows, stop - start)

        def write(tile, values):
            lanes = values.shape[1]
            mixed_ref[:, own, tile * LANES : tile * LANES + lanes] = values.reshape(
                frames, chunk, lanes
            )

        return read, write

    attend([one(index) for index in range(positions // chunk)], rows, keep)
    mixed = mixed_ref[...].reshape(tokens, INNER).astype(jnp.bfloat16)
    result = jnp.dot(mixed, output_ref[...], preferred_element_type=jnp.float32)
    hidden = after_ref[...].reshape(tokens, width).astype(jnp.float32)
    settled = (hidden + table_ref[5:6, :] * result).astype(jnp.bfloat16).astype(jnp.float32)
    normed = (layer_norm(settled) * (1.0 + table_ref[7:8, :]) + table_ref[6:7, :]).astype(
        jnp.bfloat16
    )
    predicted = dot_rows(normed, final_ref[...])
    own = pl.ds(pl.multiple_of(pl.program_id(0) * positions, positions), positions)
    predicted_ref[:, own, :] = predicted.reshape(frames, positions, predicted.shape[1])

    @pl.when(pl.program_id(0) == pl.num_programs(0) - 1)
    def _():
        if fused:
            timestep = step_ref[0]
            rate_state, rate_denoise, rate_noise = (ref[timestep] for ref in rate_refs)
            rate_state = rate_state + jnp.where(timestep == 0, 1.0, 0.0)
        for frame in range(frames):
            turned = predicted_ref[frame].T
            if fused:
                turned = (
                    rate_state * latent_ref[frame]
                    + rate_denoise * turned
                    + rate_noise * noise_ref[frame]
                )
                increment_ref[frame] = turned
                sent_ref[frame] = turned.astype(jnp.bfloat16)
            else:
                result_ref[frame] = turned


def whole(array):
    zeros = (0,) * array.ndim
    return pl.BlockSpec(array.shape, lambda step, *_: zeros, pipeline_mode=pl.Buffered(1))


def own_row(modulation):
    return pl.BlockSpec(
        (None,) + modulation.shape[1:],
        lambda step, own: (own[0], 0, 0),
        pipeline_mode=pl.Buffered(1),
    )


def cost_of(tokens, *weights):
    return pl.CostEstimate(
        flops=2 * tokens * sum(weight.size for weight in weights),
        bytes_accessed=2 * sum(weight.size for weight in weights) + 4 * tokens * weights[0].shape[-1],
        transcendentals=0,
    )


def space_block(own, latent, modulation, embed_weight, input_weight, output_weight):
    frames, channels, spatial = latent.shape
    width = embed_weight.shape[1]
    step_frames = math.gcd(frames, max(1, BLOCK_TOKENS // spatial))
    tokens = step_frames * spatial
    return pl.pallas_call(
        space_kernel,
        out_shape=jax.ShapeDtypeStruct((frames, spatial, width), jnp.bfloat16),
        grid_spec=pltpu.PrefetchScalarGridSpec(
            num_scalar_prefetch=1,
            grid=(frames // step_frames,),
            in_specs=[
                pl.BlockSpec((step_frames, channels, spatial), lambda step, own: (step, 0, 0)),
                own_row(modulation),
                whole(embed_weight),
                whole(input_weight),
                whole(output_weight),
            ],
            out_specs=pl.BlockSpec((step_frames, spatial, width), lambda step, own: (step, 0, 0)),
            scratch_shapes=[
                pltpu.VMEM((tokens, width), jnp.float32),
                pltpu.VMEM((tokens, 3 * INNER), jnp.float32),
                pltpu.VMEM((tokens, PADDED), jnp.float32),
                pltpu.VMEM((tokens, INNER), jnp.float32),
            ],
        ),
        compiler_params=pltpu.CompilerParams(vmem_limit_bytes=36 * 1024 * 1024),
        cost_estimate=cost_of(frames * spatial, input_weight, output_weight, output_weight),
        name="space_block",
    )(own, latent, modulation, embed_weight, input_weight, output_weight)


def time_block(own, after, modulation, input_weight, output_weight, final_weight, fused=()):
    frames, positions, width = after.shape
    channels = final_weight.shape[0]
    step_positions = math.gcd(positions, max(16, BLOCK_TOKENS // frames))
    shape = (frames, channels, positions)
    kinds = [jnp.float32] + [jnp.bfloat16] * bool(fused)
    return pl.pallas_call(
        functools.partial(time_kernel, bool(fused)),
        out_shape=[jax.ShapeDtypeStruct(shape, kind) for kind in kinds],
        grid_spec=pltpu.PrefetchScalarGridSpec(
            num_scalar_prefetch=1,
            grid=(positions // step_positions,),
            in_specs=[
                pl.BlockSpec((frames, step_positions, width), lambda step, own: (0, step, 0)),
                own_row(modulation),
                whole(input_weight),
                whole(output_weight),
                whole(final_weight),
            ]
            + [
                whole(array) if array.ndim > 1 else pl.BlockSpec(memory_space=pltpu.SMEM)
                for array in fused
            ],
            out_specs=[
                pl.BlockSpec(shape, lambda step, own: (0, 0, 0), pipeline_mode=pl.Buffered(1))
                for kind in kinds
            ],
            scratch_shapes=[
                pltpu.VMEM((frames, positions, channels), jnp.float32),
                pltpu.VMEM((frames, step_positions, 3 * INNER), jnp.float32),
                pltpu.VMEM((frames, step_positions, PADDED), jnp.float32),
                pltpu.VMEM((frames, step_positions, INNER), jnp.float32),
            ],
        ),
        compiler_params=pltpu.CompilerParams(vmem_limit_bytes=36 * 1024 * 1024),
        cost_estimate=cost_of(frames * positions, input_weight, output_weight, output_weight),
        name="time_block",
    )(own, after, modulation, input_weight, output_weight, final_weight, *fused)


def carry_kernel(
    last, groups, sent_ref, increment_ref, latent_ref, out_ref,
    part_ref, total_ref, plane_ref, early_ref, stage_ref, before_ref,
    part_send, part_recv, plane_send, plane_recv, stage_send, stage_recv,
):
    quarter = part_ref.shape[1]
    own = lax.axis_index("tok")
    timestep = own // groups
    plane, seat = timestep // SIDE, timestep % SIDE

    def device(plane, seat):
        return {"tok": (plane * SIDE + seat) * groups + own % groups}

    def seat_after(hop):
        return (seat + hop) % SIDE

    barrier = pltpu.get_barrier_semaphore()
    for hop in range(1, SIDE):
        for target in (device(plane, seat_after(hop)), device((plane + hop) % SIDE, seat)):
            pl.semaphore_signal(
                barrier, inc=1, device_id=target, device_id_type=pl.DeviceIdType.MESH
            )
    pl.semaphore_wait(barrier, 2 * (SIDE - 1))

    def copy(source, target, send, receive, to):
        return pltpu.make_async_remote_copy(
            src_ref=source,
            dst_ref=target,
            send_sem=send,
            recv_sem=receive,
            device_id=to,
            device_id_type=pl.DeviceIdType.MESH,
        )

    def rows_of(index):
        return pl.ds(pl.multiple_of(index * quarter, quarter), quarter)

    parts = []
    for hop in range(1, SIDE):
        seat_to = seat_after(hop)
        parts.append(
            copy(
                sent_ref.at[rows_of(seat_to)], part_ref.at[hop - 1],
                part_send.at[hop - 1], part_recv.at[hop - 1], device(plane, seat_to),
            )
        )
        parts[-1].start()
    held = [sent_ref[rows_of(seat)].astype(jnp.float32)]
    for hop in range(1, SIDE):
        parts[hop - 1].wait_recv()
        held.append(part_ref[hop - 1].astype(jnp.float32))
    total_ref[...] = functools.reduce(jnp.add, held).astype(jnp.bfloat16)
    planes = [
        copy(
            total_ref, plane_ref.at[hop - 1], plane_send.at[hop - 1], plane_recv.at[hop - 1],
            device((plane + hop) % SIDE, seat),
        )
        for hop in range(1, SIDE)
    ]
    for hop in range(1, SIDE):
        pl.when(plane + hop < SIDE)(planes[hop - 1].start)

    def earlier_seats(limit):
        total = jnp.zeros_like(held[0])
        for hop in range(SIDE):
            total = total + jnp.where((seat + SIDE - hop) % SIDE < limit, held[hop], 0.0)
        return total

    early_ref[...] = jnp.zeros_like(early_ref)
    for hop in range(1, SIDE):

        @pl.when(plane >= hop)
        def _(hop=hop):
            planes[hop - 1].wait_recv()
            early_ref[...] += plane_ref[hop - 1].astype(jnp.float32)

    early = early_ref[...]
    stages = []
    for hop in range(1, SIDE):
        seat_to = seat_after(hop)
        stage_ref[hop - 1] = early + earlier_seats(seat_to)
        stages.append(
            copy(
                stage_ref.at[hop - 1], before_ref.at[rows_of(seat)],
                stage_send.at[hop - 1], stage_recv.at[hop - 1], device(plane, seat_to),
            )
        )
        stages[-1].start()
    own_rows = rows_of(seat)

    def settle(rows, before):
        if last:
            out_ref[rows] = before + increment_ref[rows]
        else:
            out_ref[rows] = jnp.where(timestep == 0, latent_ref[rows], before)

    settle(own_rows, early + earlier_seats(seat))
    for hop in range(1, SIDE):
        stages[hop - 1].wait_recv()
        rows = rows_of((seat + SIDE - hop) % SIDE)
        settle(rows, before_ref[rows])
    for hop in range(1, SIDE):
        parts[hop - 1].wait_send()
        pl.when(plane + hop < SIDE)(planes[hop - 1].wait_send)
        stages[hop - 1].wait_send()


def carried_kernel(last, groups, sent, increment, latent):
    rows, lanes = sent.shape
    quarter = rows // SIDE
    hops = SIDE - 1
    vmem = pl.BlockSpec(memory_space=pltpu.VMEM)
    return pl.pallas_call(
        functools.partial(carry_kernel, last, groups),
        out_shape=jax.ShapeDtypeStruct((rows, lanes), jnp.float32),
        in_specs=[vmem] * 3,
        out_specs=vmem,
        scratch_shapes=[
            pltpu.VMEM((hops, quarter, lanes), jnp.bfloat16),
            pltpu.VMEM((quarter, lanes), jnp.bfloat16),
            pltpu.VMEM((hops, quarter, lanes), jnp.bfloat16),
            pltpu.VMEM((quarter, lanes), jnp.float32),
            pltpu.VMEM((hops, quarter, lanes), jnp.float32),
            pltpu.VMEM((rows, lanes), jnp.float32),
        ]
        + [pltpu.SemaphoreType.DMA((hops,))] * 6,
        compiler_params=pltpu.CompilerParams(collective_id=int(last), has_side_effects=True),
        name="carry_last" if last else "carry",
    )(sent, increment, latent)


def carried_in(last, groups, same_block, timestep, sent, increment, latent):
    rows = sent.size // LANES
    if sent.shape[-1] == LANES and rows % (SIDE * 16) == 0:
        flat = [array.reshape(rows, LANES) for array in (sent, increment, latent)]
        return carried_kernel(last, groups, *flat).reshape(latent.shape)
    gathered = lax.all_gather(
        sent, "tok", axis_index_groups=same_block if groups > 1 else None
    )
    earlier = (jnp.arange(P_SIZE) < timestep)[:, None, None, None]
    before = jnp.sum(jnp.where(earlier, gathered.astype(jnp.float32), 0.0), axis=0)
    return before + increment if last else jnp.where(timestep == 0, latent, before)


def body(
    initial_guess,
    noise_draws,
    drift_state,
    drift_denoise,
    noise_scale,
    modulation,
    embed_weight,
    space_input,
    space_output,
    time_input,
    time_output,
    final_weight,
):
    devices = lax.axis_size("tok")
    own_index = lax.axis_index("tok")
    groups = devices // P_SIZE
    timestep = own_index // groups
    own = jnp.reshape(timestep, (1,)).astype(jnp.int32)
    rates = (drift_state, drift_denoise, noise_scale)
    same_step = [[step * groups + block for block in range(groups)] for step in range(P_SIZE)]
    same_block = [[step * groups + block for step in range(P_SIZE)] for block in range(groups)]
    space_input, time_input, final_weight = space_input.T, time_input.T, final_weight.T
    latent = initial_guess
    for iteration in range(ITERS):
        after = space_block(own, latent, modulation, embed_weight, space_input, space_output)
        if groups == 1:
            increment, sent = time_block(
                own, after, modulation, time_input, time_output, final_weight,
                (latent, noise_draws) + rates,
            )
        else:
            after = lax.all_to_all(
                after, "tok", split_axis=1, concat_axis=0, axis_index_groups=same_step, tiled=True
            )
            (predicted,) = time_block(own, after, modulation, time_input, time_output, final_weight)
            predicted = lax.all_to_all(
                predicted, "tok", split_axis=0, concat_axis=2, axis_index_groups=same_step, tiled=True
            )
            rate_state, rate_denoise, rate_noise = (
                lax.dynamic_index_in_dim(rate, timestep, 0, keepdims=False) for rate in rates
            )
            rate_state = rate_state + jnp.where(timestep == 0, 1.0, 0.0)
            increment = rate_state * latent + rate_denoise * predicted + rate_noise * noise_draws
            sent = increment.astype(jnp.bfloat16)
        latent = carried_in(
            iteration == ITERS - 1, groups, same_block, timestep, sent, increment, latent
        )
    return latent


def solution(mesh):
    placed = (
        P(("group", "tok"), None, None),
        P(("group", "tok"), None, None),
        P(),
        P(),
        P(),
        P(),
        P(),
        P(),
        P(),
        P(),
        P(),
        P(),
    )
    return jax.shard_map(
        body, mesh=mesh, in_specs=placed, out_specs=P(("group", "tok"), None, None), check_vma=False
    )
```

```python
import functools
import math

import jax
import jax.numpy as jnp
from jax import lax
from jax.experimental import pallas as pl
from jax.experimental.pallas import tpu as pltpu
from jax.sharding import PartitionSpec as P

HEADS = 8
HD = 72
P_SIZE = 16
ITERS = 2
LANES = 128
INNER = HEADS * HD
PADDED = -(-INNER // LANES) * LANES
BLOCK_TOKENS = 256
SIDE = math.isqrt(P_SIZE)


def layer_norm(values):
    center = values - jnp.mean(values, -1, keepdims=True)
    return center * lax.rsqrt(jnp.mean(center * center, -1, keepdims=True) + 1e-06)


def dot_rows(values, weight_rows):
    return lax.dot_general(
        values, weight_rows, (((1,), (1,)), ((), ())), preferred_element_type=jnp.float32
    )


def head_slab(head):
    first = head * HD // LANES
    last = (head * HD + HD - 1) // LANES
    return first, last - first + 1


def part_lanes(part, tile, tiles):
    if part == 1:
        return 1, tile * LANES, (tile + tiles) * LANES
    start = part * INNER
    return 0, start + tile * LANES, start + min((tile + tiles) * LANES, INNER if part else PADDED)


def lined_keys(packed):
    low = INNER // LANES * LANES
    return pltpu.roll(packed[:, low : low + PADDED], PADDED - (INNER - low), 1)


def attend(blocks, rows, keep, lags):
    lane = lax.broadcasted_iota(jnp.int32, (rows, LANES), 1)
    open_tiles = {}
    units = [(head, place) for head in range(HEADS) for place in range(len(blocks))]

    def prepare(unit):
        head, place = unit
        read = blocks[place][0]
        tile, tiles = head_slab(head)
        low = head * HD - tile * LANES
        lanes = lax.broadcasted_iota(jnp.int32, (rows, tiles * LANES), 1)
        inside = (lanes >= low) & (lanes < low + HD)
        queries = jnp.where(inside, read(0, tile, tiles), 0.0)
        keys = jnp.where(inside, read(1, tile, tiles), 0.0)
        query_rate = lax.rsqrt(jnp.sum(queries * queries, -1, keepdims=True) / HD + 1e-06)
        key_rate = lax.rsqrt(jnp.sum(keys * keys, -1, keepdims=True) / HD + 1e-06)
        queries = (queries * (query_rate * (HD**-0.5 * math.log2(math.e)))).astype(jnp.bfloat16)
        return queries, (keys * key_rate).astype(jnp.bfloat16)

    def weigh(unit, prepared):
        weights = jnp.exp2(dot_rows(*prepared))
        if keep is not None:
            weights = jnp.where(keep, weights, 0.0)
        return weights.astype(jnp.bfloat16)

    def mix(unit, weights):
        head, place = unit
        read, write = blocks[place]
        tile, tiles = head_slab(head)
        values = read(2, tile, tiles).astype(jnp.bfloat16)
        ones = jnp.ones((rows, LANES), jnp.bfloat16)
        if tiles == 1:
            values = jnp.concatenate([values, ones], axis=1)
        mixed = jnp.dot(weights, values, preferred_element_type=jnp.float32)
        total = mixed[:, LANES:] if tiles == 1 else jnp.dot(
            weights, ones, preferred_element_type=jnp.float32
        )
        share = 1.0 / total
        for own in range(tile, tile + tiles):
            part = mixed[:, (own - tile) * LANES : min((own - tile + 1) * LANES, values.shape[1])]
            part = part * share[:, : part.shape[1]]
            if (place, own) in open_tiles:
                part = jnp.where(
                    lane >= head * HD - own * LANES, part, open_tiles.pop((place, own))
                )
            if (head + 1) * HD >= min((own + 1) * LANES, INNER):
                write(own, part)
            else:
                open_tiles[place, own] = part

    prepared, weighed = {}, {}
    for at in range(len(units) + lags[1]):
        if at < len(units):
            prepared[at] = prepare(units[at])
        if 0 <= at - lags[0] < len(units):
            weighed[at - lags[0]] = weigh(units[at - lags[0]], prepared.pop(at - lags[0]))
        if 0 <= at - lags[1] < len(units):
            mix(units[at - lags[1]], weighed.pop(at - lags[1]))


def space_kernel(
    step_ref, latent_ref, table_ref, embed_ref, input_ref, output_ref, after_ref,
    embedded_ref, packed_ref, key_ref, mixed_ref,
):
    frames, channels, spatial = latent_ref.shape
    for frame in range(frames):
        embedded_ref[frame * spatial : (frame + 1) * spatial, :] = lax.dot_general(
            latent_ref[frame].astype(jnp.bfloat16),
            embed_ref[...],
            (((0,), (0,)), ((), ())),
            preferred_element_type=jnp.float32,
        )
    normed = (
        layer_norm(embedded_ref[...]) * (1.0 + table_ref[1:2, :]) + table_ref[0:1, :]
    ).astype(jnp.bfloat16)
    packed = dot_rows(normed, input_ref[...])
    packed_ref[...] = packed
    key_ref[...] = lined_keys(packed)

    def one(frame):
        rows = slice(frame * spatial, (frame + 1) * spatial)

        def read(part, tile, tiles):
            source, start, stop = part_lanes(part, tile, tiles)
            return (packed_ref, key_ref)[source][rows, start:stop]

        def write(tile, values):
            mixed_ref[rows, tile * LANES : tile * LANES + values.shape[1]] = values

        return read, write

    attend([one(frame) for frame in range(frames)], spatial, None, (3, 6))
    result = jnp.dot(
        mixed_ref[...].astype(jnp.bfloat16), output_ref[...], preferred_element_type=jnp.float32
    )
    after = (embedded_ref[...] + table_ref[2:3, :] * result).astype(jnp.bfloat16)
    after_ref[...] = after.reshape(after_ref.shape)


def time_kernel(fused, *refs):
    step_ref, after_ref, table_ref, input_ref, output_ref, final_ref, *refs = refs
    if fused:
        latent_ref, noise_ref, *rate_refs, increment_ref, sent_ref = refs[:7]
    else:
        result_ref = refs[0]
    predicted_ref, packed_ref, key_ref, mixed_ref = refs[-4:]
    frames, positions, width = after_ref.shape
    chunk = 8
    tokens = frames * positions
    rows = frames * chunk
    hidden = after_ref[...].reshape(tokens, width).astype(jnp.float32)
    normed = (layer_norm(hidden) * (1.0 + table_ref[4:5, :]) + table_ref[3:4, :]).astype(
        jnp.bfloat16
    )
    packed = dot_rows(normed, input_ref[...])
    packed_ref[...] = packed.reshape(packed_ref.shape)
    key_ref[...] = lined_keys(packed).reshape(key_ref.shape)
    keep = (lax.broadcasted_iota(jnp.int32, (rows, rows), 0) % chunk) == (
        lax.broadcasted_iota(jnp.int32, (rows, rows), 1) % chunk
    )

    def one(index):
        own = slice(index * chunk, (index + 1) * chunk)

        def read(part, tile, tiles):
            source, start, stop = part_lanes(part, tile, tiles)
            return (packed_ref, key_ref)[source][:, own, start:stop].reshape(rows, stop - start)

        def write(tile, values):
            lanes = values.shape[1]
            mixed_ref[:, own, tile * LANES : tile * LANES + lanes] = values.reshape(
                frames, chunk, lanes
            )

        return read, write

    attend([one(index) for index in range(positions // chunk)], rows, keep, (4, 8))
    mixed = mixed_ref[...].reshape(tokens, INNER).astype(jnp.bfloat16)
    result = jnp.dot(mixed, output_ref[...], preferred_element_type=jnp.float32)
    hidden = after_ref[...].reshape(tokens, width).astype(jnp.float32)
    settled = (hidden + table_ref[5:6, :] * result).astype(jnp.bfloat16).astype(jnp.float32)
    normed = (layer_norm(settled) * (1.0 + table_ref[7:8, :]) + table_ref[6:7, :]).astype(
        jnp.bfloat16
    )
    predicted = dot_rows(normed, final_ref[...])
    own = pl.ds(pl.multiple_of(pl.program_id(0) * positions, positions), positions)
    predicted_ref[:, own, :] = predicted.reshape(frames, positions, predicted.shape[1])

    @pl.when(pl.program_id(0) == pl.num_programs(0) - 1)
    def _():
        if fused:
            timestep = step_ref[0]
            rate_state, rate_denoise, rate_noise = (ref[timestep] for ref in rate_refs)
            rate_state = rate_state + jnp.where(timestep == 0, 1.0, 0.0)
        for frame in range(frames):
            turned = predicted_ref[frame].T
            if fused:
                turned = (
                    rate_state * latent_ref[frame]
                    + rate_denoise * turned
                    + rate_noise * noise_ref[frame]
                )
                increment_ref[frame] = turned
                sent_ref[frame] = turned.astype(jnp.bfloat16)
            else:
                result_ref[frame] = turned


def whole(array):
    zeros = (0,) * array.ndim
    return pl.BlockSpec(array.shape, lambda step, *_: zeros, pipeline_mode=pl.Buffered(1))


def own_row(modulation):
    return pl.BlockSpec(
        (None,) + modulation.shape[1:],
        lambda step, own: (own[0], 0, 0),
        pipeline_mode=pl.Buffered(1),
    )


def cost_of(tokens, *weights):
    return pl.CostEstimate(
        flops=2 * tokens * sum(weight.size for weight in weights),
        bytes_accessed=2 * sum(weight.size for weight in weights) + 4 * tokens * weights[0].shape[-1],
        transcendentals=0,
    )


def space_block(own, latent, modulation, embed_weight, input_weight, output_weight):
    frames, channels, spatial = latent.shape
    width = embed_weight.shape[1]
    step_frames = math.gcd(frames, max(1, BLOCK_TOKENS // spatial))
    tokens = step_frames * spatial
    return pl.pallas_call(
        space_kernel,
        out_shape=jax.ShapeDtypeStruct((frames, spatial, width), jnp.bfloat16),
        grid_spec=pltpu.PrefetchScalarGridSpec(
            num_scalar_prefetch=1,
            grid=(frames // step_frames,),
            in_specs=[
                pl.BlockSpec((step_frames, channels, spatial), lambda step, own: (step, 0, 0)),
                own_row(modulation),
                whole(embed_weight),
                whole(input_weight),
                whole(output_weight),
            ],
            out_specs=pl.BlockSpec((step_frames, spatial, width), lambda step, own: (step, 0, 0)),
            scratch_shapes=[
                pltpu.VMEM((tokens, width), jnp.float32),
                pltpu.VMEM((tokens, 3 * INNER), jnp.float32),
                pltpu.VMEM((tokens, PADDED), jnp.float32),
                pltpu.VMEM((tokens, INNER), jnp.float32),
            ],
        ),
        compiler_params=pltpu.CompilerParams(vmem_limit_bytes=60 * 1024 * 1024),
        cost_estimate=cost_of(frames * spatial, input_weight, output_weight, output_weight),
        name="space_block",
    )(own, latent, modulation, embed_weight, input_weight, output_weight)


def time_block(own, after, modulation, input_weight, output_weight, final_weight, fused=()):
    frames, positions, width = after.shape
    channels = final_weight.shape[0]
    step_positions = math.gcd(positions, max(16, BLOCK_TOKENS // frames))
    shape = (frames, channels, positions)
    kinds = [jnp.float32] + [jnp.bfloat16] * bool(fused)
    return pl.pallas_call(
        functools.partial(time_kernel, bool(fused)),
        out_shape=[jax.ShapeDtypeStruct(shape, kind) for kind in kinds],
        grid_spec=pltpu.PrefetchScalarGridSpec(
            num_scalar_prefetch=1,
            grid=(positions // step_positions,),
            in_specs=[
                pl.BlockSpec((frames, step_positions, width), lambda step, own: (0, step, 0)),
                own_row(modulation),
                whole(input_weight),
                whole(output_weight),
                whole(final_weight),
            ]
            + [
                whole(array) if array.ndim > 1 else pl.BlockSpec(memory_space=pltpu.SMEM)
                for array in fused
            ],
            out_specs=[
                pl.BlockSpec(shape, lambda step, own: (0, 0, 0), pipeline_mode=pl.Buffered(1))
                for kind in kinds
            ],
            scratch_shapes=[
                pltpu.VMEM((frames, positions, channels), jnp.float32),
                pltpu.VMEM((frames, step_positions, 3 * INNER), jnp.float32),
                pltpu.VMEM((frames, step_positions, PADDED), jnp.float32),
                pltpu.VMEM((frames, step_positions, INNER), jnp.float32),
            ],
        ),
        compiler_params=pltpu.CompilerParams(vmem_limit_bytes=60 * 1024 * 1024),
        cost_estimate=cost_of(frames * positions, input_weight, output_weight, output_weight),
        name="time_block",
    )(own, after, modulation, input_weight, output_weight, final_weight, *fused)


def carry_kernel(
    last, groups, sent_ref, increment_ref, latent_ref, out_ref,
    part_ref, total_ref, plane_ref, early_ref, stage_ref, before_ref,
    part_send, part_recv, plane_send, plane_recv, stage_send, stage_recv,
):
    quarter = part_ref.shape[1]
    own = lax.axis_index("tok")
    timestep = own // groups
    plane, seat = timestep // SIDE, timestep % SIDE

    def device(plane, seat):
        return {"tok": (plane * SIDE + seat) * groups + own % groups}

    def seat_after(hop):
        return (seat + hop) % SIDE

    barrier = pltpu.get_barrier_semaphore()
    for hop in range(1, SIDE):
        for target in (device(plane, seat_after(hop)), device((plane + hop) % SIDE, seat)):
            pl.semaphore_signal(
                barrier, inc=1, device_id=target, device_id_type=pl.DeviceIdType.MESH
            )
    pl.semaphore_wait(barrier, 2 * (SIDE - 1))

    def copy(source, target, send, receive, to):
        return pltpu.make_async_remote_copy(
            src_ref=source,
            dst_ref=target,
            send_sem=send,
            recv_sem=receive,
            device_id=to,
            device_id_type=pl.DeviceIdType.MESH,
        )

    def rows_of(index):
        return pl.ds(pl.multiple_of(index * quarter, quarter), quarter)

    parts = []
    for hop in range(1, SIDE):
        seat_to = seat_after(hop)
        parts.append(
            copy(
                sent_ref.at[rows_of(seat_to)], part_ref.at[hop - 1],
                part_send.at[hop - 1], part_recv.at[hop - 1], device(plane, seat_to),
            )
        )
        parts[-1].start()
    held = [sent_ref[rows_of(seat)].astype(jnp.float32)]
    for hop in range(1, SIDE):
        parts[hop - 1].wait_recv()
        held.append(part_ref[hop - 1].astype(jnp.float32))
    total_ref[...] = functools.reduce(jnp.add, held).astype(jnp.bfloat16)
    planes = [
        copy(
            total_ref, plane_ref.at[hop - 1], plane_send.at[hop - 1], plane_recv.at[hop - 1],
            device((plane + hop) % SIDE, seat),
        )
        for hop in range(1, SIDE)
    ]
    for hop in range(1, SIDE):
        pl.when(plane + hop < SIDE)(planes[hop - 1].start)

    def earlier_seats(limit):
        total = jnp.zeros_like(held[0])
        for hop in range(SIDE):
            total = total + jnp.where((seat + SIDE - hop) % SIDE < limit, held[hop], 0.0)
        return total

    early_ref[...] = jnp.zeros_like(early_ref)
    for hop in range(1, SIDE):

        @pl.when(plane >= hop)
        def _(hop=hop):
            planes[hop - 1].wait_recv()
            early_ref[...] += plane_ref[hop - 1].astype(jnp.float32)

    early = early_ref[...]
    stages = []
    for hop in range(1, SIDE):
        seat_to = seat_after(hop)
        stage_ref[hop - 1] = early + earlier_seats(seat_to)
        stages.append(
            copy(
                stage_ref.at[hop - 1], before_ref.at[rows_of(seat)],
                stage_send.at[hop - 1], stage_recv.at[hop - 1], device(plane, seat_to),
            )
        )
        stages[-1].start()
    own_rows = rows_of(seat)

    def settle(rows, before):
        if last:
            out_ref[rows] = before + increment_ref[rows]
        else:
            out_ref[rows] = jnp.where(timestep == 0, latent_ref[rows], before)

    settle(own_rows, early + earlier_seats(seat))
    for hop in range(1, SIDE):
        stages[hop - 1].wait_recv()
        rows = rows_of((seat + SIDE - hop) % SIDE)
        settle(rows, before_ref[rows])
    for hop in range(1, SIDE):
        parts[hop - 1].wait_send()
        pl.when(plane + hop < SIDE)(planes[hop - 1].wait_send)
        stages[hop - 1].wait_send()


def carried_kernel(last, groups, sent, increment, latent):
    rows, lanes = sent.shape
    quarter = rows // SIDE
    hops = SIDE - 1
    vmem = pl.BlockSpec(memory_space=pltpu.VMEM)
    return pl.pallas_call(
        functools.partial(carry_kernel, last, groups),
        out_shape=jax.ShapeDtypeStruct((rows, lanes), jnp.float32),
        in_specs=[vmem] * 3,
        out_specs=vmem,
        scratch_shapes=[
            pltpu.VMEM((hops, quarter, lanes), jnp.bfloat16),
            pltpu.VMEM((quarter, lanes), jnp.bfloat16),
            pltpu.VMEM((hops, quarter, lanes), jnp.bfloat16),
            pltpu.VMEM((quarter, lanes), jnp.float32),
            pltpu.VMEM((hops, quarter, lanes), jnp.float32),
            pltpu.VMEM((rows, lanes), jnp.float32),
        ]
        + [pltpu.SemaphoreType.DMA((hops,))] * 6,
        compiler_params=pltpu.CompilerParams(collective_id=int(last), has_side_effects=True),
        name="carry_last" if last else "carry",
    )(sent, increment, latent)


def carried_in(last, groups, same_block, timestep, sent, increment, latent):
    rows = sent.size // LANES
    if sent.shape[-1] == LANES and rows % (SIDE * 16) == 0:
        flat = [array.reshape(rows, LANES) for array in (sent, increment, latent)]
        return carried_kernel(last, groups, *flat).reshape(latent.shape)
    gathered = lax.all_gather(
        sent, "tok", axis_index_groups=same_block if groups > 1 else None
    )
    earlier = (jnp.arange(P_SIZE) < timestep)[:, None, None, None]
    before = jnp.sum(jnp.where(earlier, gathered.astype(jnp.float32), 0.0), axis=0)
    return before + increment if last else jnp.where(timestep == 0, latent, before)


def body(
    initial_guess,
    noise_draws,
    drift_state,
    drift_denoise,
    noise_scale,
    modulation,
    embed_weight,
    space_input,
    space_output,
    time_input,
    time_output,
    final_weight,
):
    devices = lax.axis_size("tok")
    own_index = lax.axis_index("tok")
    groups = devices // P_SIZE
    timestep = own_index // groups
    own = jnp.reshape(timestep, (1,)).astype(jnp.int32)
    rates = (drift_state, drift_denoise, noise_scale)
    same_step = [[step * groups + block for block in range(groups)] for step in range(P_SIZE)]
    same_block = [[step * groups + block for step in range(P_SIZE)] for block in range(groups)]
    space_input, time_input, final_weight = space_input.T, time_input.T, final_weight.T
    latent = initial_guess
    for iteration in range(ITERS):
        after = space_block(own, latent, modulation, embed_weight, space_input, space_output)
        if groups == 1:
            increment, sent = time_block(
                own, after, modulation, time_input, time_output, final_weight,
                (latent, noise_draws) + rates,
            )
        else:
            after = lax.all_to_all(
                after, "tok", split_axis=1, concat_axis=0, axis_index_groups=same_step, tiled=True
            )
            (predicted,) = time_block(own, after, modulation, time_input, time_output, final_weight)
            predicted = lax.all_to_all(
                predicted, "tok", split_axis=0, concat_axis=2, axis_index_groups=same_step, tiled=True
            )
            rate_state, rate_denoise, rate_noise = (
                lax.dynamic_index_in_dim(rate, timestep, 0, keepdims=False) for rate in rates
            )
            rate_state = rate_state + jnp.where(timestep == 0, 1.0, 0.0)
            increment = rate_state * latent + rate_denoise * predicted + rate_noise * noise_draws
            sent = increment.astype(jnp.bfloat16)
        latent = carried_in(
            iteration == ITERS - 1, groups, same_block, timestep, sent, increment, latent
        )
    return latent


def solution(mesh):
    placed = (
        P(("group", "tok"), None, None),
        P(("group", "tok"), None, None),
        P(),
        P(),
        P(),
        P(),
        P(),
        P(),
        P(),
        P(),
        P(),
        P(),
    )
    return jax.shard_map(
        body, mesh=mesh, in_specs=placed, out_specs=P(("group", "tok"), None, None), check_vma=False
    )
```
